32 devices in a mesh: row: 16 (over z, y, core), col: 2 (over x).
Axes of the slice: x: 2, y: 2, z: 4, core: 2. Of those that a mesh axis runs over, the one named last changes fastest.
Arguments:
- seq: float32 [768, 1024], P('row', 'col'), may hold values from -6 to 6
- query: float32 [768, 1024], P('row', 'col'), may hold values from -24 to 24, as said below
- key: float32 [768, 1024], P('col', 'row'), may hold values from -24 to 24, as said below
- value: float32 [768, 1024], P('col', 'row'), may hold values from -6 to 6
- pair: float32 [768, 768, 128], P('row', 'col'), may hold values from -6 to 6
- w_bias: float32 [128, 32], replicated, may hold values from -0.5 to 0.5
- w_out: float32 [1024, 1024], P(None, 'col'), may hold values from -0.75 to 0.75
- w_left: float32 [1024, 64], P('col'), may hold values from -0.1875 to 0.1875
- w_right: float32 [1024, 64], P('col'), may hold values from -0.1875 to 0.1875
- w_outer: float32 [128, 128], replicated, may hold values from -0.5 to 0.5
- outer_bias: float32 [128], replicated, may hold values from -3 to 3
- w_up: float32 [128, 512], replicated, may hold values from -0.5 to 0.5
- w_down: float32 [512, 128], replicated, may hold values from -0.25 to 0.25
Outputs:
- seq_new: float32 [768, 1024], P('row', 'col')
- pair_new: float32 [768, 768, 128], P('row', 'col')
The draws below stay inside these ranges and needn't reach their ends.
Inputs may be any that keep to these rules, and one draw needn't show every extreme that they name: `query`: Head-major queries of order one; some residues may be much larger. `key`: Head-major keys of order one; some residues may be much larger.
All inputs are finite; a program needn't handle non-finite values.
Results may differ from the reference program's by a relative error of at most 0.0003.
Values sent between devices are 32-bit elements; how exact they have to be, the bound alone decides.
A program may use at most 128 MiB of HBM per device.

```python
import jax
import jax.numpy as jnp
from jax import lax

HEADS = 32
CP = 128
PAIR_HIDDEN = 512
OPD = 64
RES = 48
D = 1024
RESIDUES = 768
N_ROW = 16


def draw_shared(key):
    base = jax.random.fold_in(key, 77)
    first, second = jax.random.split(base, 2)
    queries = jnp.clip(jax.random.normal(first, (RESIDUES, D), jnp.float32), -6.0, 6.0)
    keys_drawn = jnp.clip(jax.random.normal(second, (RESIDUES, D), jnp.float32), -6.0, 6.0)
    return (queries, keys_drawn)


def draw_query(key, part):
    return draw_shared(key)[0]


def draw_key(key, part):
    return draw_shared(key)[1]


def block_levels(key, dims, shards, least, largest):
    def one(position, shards_of):
        steps = jax.random.uniform(jax.random.fold_in(jax.random.fold_in(key, 6), position), (shards_of,), jnp.float32, least / len(shards), largest / len(shards))
        return jnp.repeat(jnp.exp(steps), dims[position] // shards_of).reshape((-1,) + (1,) * (len(dims) - position - 1))

    gain = one(*shards[0])
    for cut in shards[1:]:
        gain = gain * one(*cut)
    return gain


def noise(own_key, extent, deviation, bound, shards=(), dtype=jnp.bfloat16):
    level = block_levels(own_key, extent, shards, -0.22, 0.18) if shards else 1.0
    drawn = jax.random.normal(own_key, extent, jnp.float32) * deviation * level
    return jnp.minimum(jnp.maximum(drawn, -bound), bound).astype(dtype)


def setup_inputs(seed: int = 0) -> dict:
    splits = jax.random.split(jax.random.key(seed), 14)
    seq = noise(splits[0], (RESIDUES, D), 1.0, 6.0, ((0, 16), (1, 2)), jnp.float32)
    query = draw_query(jax.random.fold_in(splits[13], 71), 0)
    key = draw_key(jax.random.fold_in(splits[13], 71), 0)
    value = noise(splits[3], (RESIDUES, D), 1.0, 6.0, ((0, 2), (1, 16)), jnp.float32)
    pair = noise(splits[4], (RESIDUES, RESIDUES, CP), 1.0, 6.0, ((0, 16), (1, 2)), jnp.float32)
    w_bias = noise(splits[5], (CP, HEADS), CP ** -0.5, 0.5, (), jnp.float32)
    w_out = noise(splits[6], (D, D), (D // 16) ** -0.5, 0.75, ((1, 2),), jnp.float32)
    w_left = noise(splits[7], (D, OPD), D ** -0.5, 0.1875, ((0, 2),), jnp.float32)
    w_right = noise(splits[8], (D, OPD), D ** -0.5, 0.1875, ((0, 2),), jnp.float32)
    w_outer = noise(splits[9], (2 * OPD, CP), (2 * OPD) ** -0.5, 0.5, (), jnp.float32)
    outer_bias = noise(splits[10], (CP,), 0.5, 3.0, (), jnp.float32)
    w_up = noise(splits[11], (CP, PAIR_HIDDEN), CP ** -0.5, 0.5, (), jnp.float32)
    w_down = noise(splits[12], (PAIR_HIDDEN, CP), PAIR_HIDDEN ** -0.5, 0.25, (), jnp.float32)
    return {"seq": seq, "query": query, "key": key, "value": value, "pair": pair, "w_bias": w_bias, "w_out": w_out, "w_left": w_left, "w_right": w_right, "w_outer": w_outer, "outer_bias": outer_bias, "w_up": w_up, "w_down": w_down}


HIGH = lax.Precision.HIGHEST

def channel_norm(x):
    centre = x - lax.optimization_barrier(jnp.mean(x, axis=-1, keepdims=True))
    return centre * lax.rsqrt(lax.optimization_barrier(jnp.mean(centre * centre, axis=-1, keepdims=True)) + 1e-05)

def reference(seq, query, key, value, pair, w_bias, w_out, w_left, w_right, w_outer, outer_bias, w_up, w_down):
    residues = seq.shape[0]
    heads = w_bias.shape[1]
    head_dim = seq.shape[1] // heads
    proj_width = w_left.shape[1]
    blocks = pair.reshape(N_ROW, RES, residues, pair.shape[2])

    def make_bias(block):
        return jnp.einsum('ijc,ch->ihj', channel_norm(block), w_bias, precision=HIGH)
    bias = lax.map(make_bias, blocks).reshape(residues, heads, residues)
    q_heads = query.reshape(residues, heads, head_dim)
    k_heads = key.reshape(residues, heads, head_dim)
    v_heads = value.reshape(residues, heads, head_dim)
    scores = jnp.einsum('ihd,jhd->ihj', q_heads, k_heads, precision=HIGH) / jnp.sqrt(jnp.float32(head_dim)) + bias
    weights = jax.nn.softmax(scores, axis=-1)
    attn = jnp.einsum('ihj,jhd->ihd', weights, v_heads, precision=HIGH).reshape(residues, heads * head_dim)
    seq_new = seq + jnp.dot(attn, w_out, precision=HIGH)
    mean_value = lax.optimization_barrier(jnp.mean(seq_new, axis=1, keepdims=True))
    mean_square = lax.optimization_barrier(jnp.mean(seq_new * seq_new, axis=1, keepdims=True))
    seq_norm = (seq_new - mean_value) * lax.rsqrt(mean_square - mean_value * mean_value + 1e-05)
    left = jnp.dot(seq_norm, w_left, precision=HIGH)
    right = jnp.dot(seq_norm, w_right, precision=HIGH)
    w_prod = w_outer[:proj_width]
    w_diff = w_outer[proj_width:]
    table = right[:, :, None] * w_prod[None, :, :]
    right_diff = jnp.dot(right, w_diff, precision=HIGH)
    left_diff = jnp.dot(left, w_diff, precision=HIGH)
    left_blocks = left.reshape(N_ROW, RES, proj_width)
    left_diff_blocks = left_diff.reshape(N_ROW, RES, left_diff.shape[1])

    def update(args):
        block, left_block, diff_block = args
        outer = jnp.einsum('ip,jpc->ijc', left_block, table, precision=HIGH) + diff_block[:, None, :] - right_diff[None, :, :] + outer_bias
        mid = block + outer
        hidden_act = jax.nn.relu(jnp.einsum('ijc,ck->ijk', channel_norm(mid), w_up, precision=HIGH))
        return mid + jnp.einsum('ijk,kc->ijc', hidden_act, w_down, precision=HIGH)
    pair_new = lax.map(update, (blocks, left_blocks, left_diff_blocks)).reshape(pair.shape)
    return (seq_new, pair_new)
```

```python
import functools

import jax
import jax.numpy as jnp
from jax import lax
from jax.experimental import pallas as pl
from jax.experimental.pallas import tpu as pltpu
from jax.sharding import PartitionSpec as P

HIGH = lax.Precision.HIGHEST
F32 = jnp.float32
BF16 = jnp.bfloat16
VMEM_LIMIT = 60 * 1024 * 1024


def halves(x):
    high = x.astype(BF16)
    low = (x - high.astype(F32)).astype(BF16)
    return high, low


def split(x):
    kept = lax.reduce_precision(x, 8, 7)
    return kept.astype(BF16), (x - kept).astype(BF16)


def channel_norm(x):
    centre = x - jnp.mean(x, axis=-1, keepdims=True)
    return centre * lax.rsqrt(jnp.mean(centre * centre, axis=-1, keepdims=True) + 1e-05)


def dot_nt(a, b, precision=None):
    return lax.dot_general(
        a, b, (((1,), (1,)), ((), ())), precision=precision, preferred_element_type=F32
    )


def bias_kernel(pair_ref, wt_hi_ref, wt_lo_ref, out_ref):
    group = pair_ref.shape[0]
    rows = [halves(channel_norm(pair_ref[i])) for i in range(group)]
    high = jnp.concatenate([r[0] for r in rows], axis=1)
    low = jnp.concatenate([r[1] for r in rows], axis=1)
    wt_hi = wt_hi_ref[...]
    flat = dot_nt(wt_hi, high) + (dot_nt(wt_hi, low) + dot_nt(wt_lo_ref[...], high))
    out_ref[...] = flat.reshape(out_ref.shape)


def pair_bias(pair, w_bias):
    rows, cols, channels = pair.shape
    heads = w_bias.shape[1]
    group = 8
    eye = jnp.eye(group, dtype=F32)
    wt = (w_bias.T[:, None, None, :] * eye[None, :, :, None]).reshape(
        heads * group, group * channels
    )
    wt_hi, wt_lo = split(wt)
    whole = pl.BlockSpec((heads * group, group * channels), lambda i: (0, 0))
    return pl.pallas_call(
        bias_kernel,
        out_shape=jax.ShapeDtypeStruct((heads, rows, cols), F32),
        grid=(rows // group,),
        in_specs=[pl.BlockSpec((group, cols, channels), lambda i: (i, 0, 0)), whole, whole],
        out_specs=pl.BlockSpec((heads, group, cols), lambda i: (0, i, 0)),
        compiler_params=pltpu.CompilerParams(vmem_limit_bytes=VMEM_LIMIT),
        name="pair_bias",
    )(pair, wt_hi, wt_lo)


def attention_kernel(head_dim, q_ref, k_ref, v_ref, bias_ref, part_ref, top_ref, total_ref):
    rows = q_ref.shape[0]
    heads = bias_ref.shape[0]
    per = 128 // head_dim
    scale = F32(head_dim) ** -0.5
    lane = lax.broadcasted_iota(jnp.int32, (rows, 128), 1)
    tops = jnp.zeros((rows, 128), F32)
    totals = jnp.zeros((rows, 128), F32)
    for g in range(heads // per):
        lanes = slice(g * 128, (g + 1) * 128)
        q = q_ref[:, lanes]
        q4 = jnp.concatenate(
            [jnp.where(lane // head_dim == m, q, 0.0) for m in range(per)], axis=0
        )
        bias = bias_ref[g * per : (g + 1) * per].reshape(per * rows, -1)
        scores = dot_nt(q4, k_ref[:, lanes], HIGH) * scale + bias
        top = jnp.max(scores, axis=1, keepdims=True)
        expo = jnp.exp(scores - top)
        total = jnp.sum(expo, axis=1, keepdims=True)
        e_hi, e_lo = halves(expo)
        v_hi, v_lo = halves(v_ref[:, lanes])
        dot = functools.partial(jnp.dot, preferred_element_type=F32)
        out = dot(e_hi, v_hi) + (dot(e_hi, v_lo) + dot(e_lo, v_hi))
        part = jnp.zeros((rows, 128), F32)
        for m in range(per):
            mine = slice(m * rows, (m + 1) * rows)
            part = jnp.where(lane // head_dim == m, out[mine], part)
            tops = jnp.where(lane == g * per + m, top[mine], tops)
            totals = jnp.where(lane == g * per + m, total[mine], totals)
        part_ref[:, lanes] = part
    top_ref[...] = tops
    total_ref[...] = totals


def attention(q, k, v, bias, head_dim):
    rows, width = q.shape
    small = jax.ShapeDtypeStruct((rows, 128), F32)
    return pl.pallas_call(
        functools.partial(attention_kernel, head_dim),
        out_shape=(jax.ShapeDtypeStruct((rows, width), F32), small, small),
        compiler_params=pltpu.CompilerParams(vmem_limit_bytes=VMEM_LIMIT),
        name="attention",
    )(q, k, v, bias)


def transition_kernel(
    pair_ref, left_ref, right_ref, w_outer_ref, bias_ref, up_ref, down_ref, down_hi_ref, out_ref,
    left_t, right_s, left_d,
):
    step = pl.program_id(0)
    group, cols, channels = pair_ref.shape
    proj = left_ref.shape[1]
    dot = functools.partial(jnp.dot, preferred_element_type=F32)

    @pl.when(step == 0)
    def _():
        left = left_ref[...]
        left_t[...] = left.T
        left_d[...] = jnp.dot(left, w_outer_ref[proj:], precision=HIGH) + bias_ref[...]
        r_hi, r_lo = halves(right_ref[...])
        right_s[...] = jnp.concatenate([r_hi, r_lo, r_hi], axis=1)

    lane = lax.broadcasted_iota(jnp.int32, left_t.shape, 1)
    w_prod = w_outer_ref[:proj]
    w_diff = w_outer_ref[proj:]
    weights = []
    for g in range(group):
        column = jnp.sum(
            jnp.where(lane == step * group + g, left_t[...], 0.0), axis=1, keepdims=True
        )
        w_hi, w_lo = halves(column * w_prod - w_diff)
        weights.append(jnp.concatenate([w_hi, w_hi, w_lo], axis=0))
    outer = dot(right_s[...], jnp.concatenate(weights, axis=1))
    for g in range(group):
        mid = pair_ref[g] + (
            outer[:, g * channels : (g + 1) * channels]
            + left_d[pl.ds(step * group + g, 1), :]
        )
        x_hi, x_lo = halves(channel_norm(mid))
        hidden = jnp.maximum(dot(jnp.concatenate([x_hi, x_lo, x_hi], axis=1), up_ref[...]), 0.0)
        h_hi, h_lo = halves(hidden)
        both = dot(h_hi, down_ref[...])
        out_ref[g] = mid + (
            both[:, :channels] + (both[:, channels:] + dot(h_lo, down_hi_ref[...]))
        )


def transition(pair, left, right, w_outer, outer_bias, w_up, w_down):
    rows, cols, channels = pair.shape
    proj = left.shape[1]
    hidden = w_up.shape[1]
    group = 2
    up_hi, up_lo = split(w_up)
    up = jnp.concatenate([up_hi, up_hi, up_lo], axis=0)
    down_hi, down_lo = split(w_down)
    down = jnp.concatenate([down_hi, down_lo], axis=1)

    def whole(x):
        return pl.BlockSpec(x.shape, lambda i: (0,) * x.ndim)

    block = pl.BlockSpec((group, cols, channels), lambda i: (i, 0, 0))
    fixed = (left, right, w_outer, outer_bias.reshape(1, channels), up, down, down_hi)
    return pl.pallas_call(
        transition_kernel,
        out_shape=jax.ShapeDtypeStruct(pair.shape, F32),
        grid=(rows // group,),
        in_specs=[block] + [whole(x) for x in fixed],
        out_specs=block,
        scratch_shapes=[
            pltpu.VMEM((proj, rows), F32),
            pltpu.VMEM((cols, 3 * proj), BF16),
            pltpu.VMEM((rows, channels), F32),
        ],
        compiler_params=pltpu.CompilerParams(vmem_limit_bytes=VMEM_LIMIT),
        name="transition",
    )(pair, *fixed)


def per_device(
    seq, query, key, value, pair, w_bias, w_out, w_left, w_right, w_outer, outer_bias, w_up, w_down
):
    rows, cols, channels = pair.shape
    heads = w_bias.shape[1]
    width = w_out.shape[0]
    head_dim = width // heads
    proj = w_left.shape[1]
    queries = lax.all_gather(query, "col", axis=1, tiled=True)
    keys = lax.all_gather(key, "row", axis=1, tiled=True)
    values = lax.all_gather(value, "row", axis=1, tiled=True)
    bias = pair_bias(pair, w_bias)
    part, top, total = attention(queries, keys, values, bias, head_dim)
    every = lax.all_gather(
        jnp.concatenate([part, top[:, :heads], total[:, :heads]], axis=1), "col"
    )
    parts = every[:, :, :width]
    tops = every[:, :, width : width + heads]
    totals = every[:, :, width + heads :]
    scale = jnp.exp(tops - jnp.max(tops, axis=0))
    scale = scale / jnp.sum(scale * totals, axis=0)
    attn = jnp.sum(parts * jnp.repeat(scale, head_dim, axis=2), axis=0)
    seq_new = seq + jnp.dot(attn, w_out, precision=HIGH)
    here = seq.shape[1]
    local_mean = jnp.mean(seq_new, axis=1, keepdims=True)
    centred = seq_new - local_mean
    w_both = jnp.concatenate([w_left, w_right], axis=1)
    projected = jnp.dot(centred, w_both, precision=HIGH)
    spread = jnp.sum(centred * centred, axis=1, keepdims=True)
    column = jnp.broadcast_to(jnp.sum(w_both, axis=0, keepdims=True), (rows, 2 * proj))
    sent = jnp.concatenate([projected, column, local_mean, spread], axis=1)
    every = lax.all_gather(sent, "col")
    means = every[:, :, 4 * proj : 4 * proj + 1]
    spreads = every[:, :, 4 * proj + 1 :]
    mean = jnp.mean(means, axis=0)
    offset = means - mean
    variance = (jnp.sum(spreads, axis=0) + here * jnp.sum(offset * offset, axis=0)) / width
    both = jnp.sum(every[:, :, : 2 * proj] + offset * every[:, :, 2 * proj : 4 * proj], axis=0)
    both = both * lax.rsqrt(variance + 1e-05)
    left = both[:, :proj]
    right_every = lax.all_gather(both[:, proj:], "row", axis=0, tiled=True)
    right = lax.dynamic_slice_in_dim(right_every, lax.axis_index("col") * cols, cols, 0)
    pair_new = transition(pair, left, right, w_outer, outer_bias, w_up, w_down)
    return seq_new, pair_new


def solution(mesh):
    in_specs = (
        P("row", "col"),
        P("row", "col"),
        P("col", "row"),
        P("col", "row"),
        P("row", "col", None),
        P(),
        P(None, "col"),
        P("col", None),
        P("col", None),
        P(),
        P(),
        P(),
        P(),
    )
    out_specs = (P("row", "col"), P("row", "col", None))
    return jax.shard_map(
        per_device, mesh=mesh, in_specs=in_specs, out_specs=out_specs, check_vma=False
    )
```

```python
import functools

import jax
import jax.numpy as jnp
from jax import lax
from jax.experimental import pallas as pl
from jax.experimental.pallas import tpu as pltpu
from jax.sharding import PartitionSpec as P

HIGH = lax.Precision.HIGHEST
F32 = jnp.float32
BF16 = jnp.bfloat16
VMEM_LIMIT = 60 * 1024 * 1024
MESH = pl.DeviceIdType.MESH


def halves(x):
    high = x.astype(BF16)
    low = (x - high.astype(F32)).astype(BF16)
    return high, low


def split(x):
    kept = lax.reduce_precision(x, 8, 7)
    return kept.astype(BF16), (x - kept).astype(BF16)


def channel_norm(x):
    centre = x - jnp.mean(x, axis=-1, keepdims=True)
    return centre * lax.rsqrt(jnp.mean(centre * centre, axis=-1, keepdims=True) + 1e-05)


def dot_nt(a, b, precision=None):
    return lax.dot_general(
        a, b, (((1,), (1,)), ((), ())), precision=precision, preferred_element_type=F32
    )


def gather_attention_kernel(
    n, n_col, head_dim, heads,
    kv_ref, q_ref, pair_ref, wt_hi_ref, wt_lo_ref,
    part_ref, stat_ref,
    kv_buf, q_buf, bias_buf, pair_buf,
    recv_sem, z_sem, y_sem, core_sem, q_send, q_recv, pair_sem,
):
    n_z = n // 4
    n_slot, rows, wide = q_ref.shape
    groups, group = pair_buf.shape[:2]
    per = wide // 2 // head_dim
    row, col = lax.axis_index("row"), lax.axis_index("col")
    core, y = lax.rem(row, 2), lax.rem(lax.div(row, 2), 2)
    core_peer, y_peer = row + 1 - 2 * core, row + 2 - 4 * y
    z_peers = [lax.rem(row + 4 * k, n) for k in range(1, n_z)]
    col_peers = [lax.rem(col + k, n_col) for k in range(1, n_col)]

    def pair_copy(g):
        return pltpu.make_async_copy(
            pair_ref.at[pl.ds(g * group, group)], pair_buf.at[g], pair_sem.at[g]
        )

    for g in range(groups):
        pair_copy(g).start()
    own_kv = pltpu.make_async_copy(kv_ref, kv_buf.at[row], recv_sem.at[row])
    own_kv.start()
    own_q = pltpu.make_async_copy(
        q_ref, q_buf.at[pl.ds(col * n_slot, n_slot)], q_recv.at[col]
    )
    own_q.start()

    barrier = pltpu.get_barrier_semaphore()
    for peer in z_peers + [y_peer, core_peer]:
        pl.semaphore_signal(barrier, inc=1, device_id={"row": peer}, device_id_type=MESH)
    for peer in col_peers:
        pl.semaphore_signal(barrier, inc=1, device_id={"col": peer}, device_id_type=MESH)
    pl.semaphore_wait(barrier, n_z + n_col)

    def put(src, slot, sem, peer):
        return pltpu.make_async_remote_copy(
            src_ref=src,
            dst_ref=kv_buf.at[slot],
            send_sem=sem,
            recv_sem=recv_sem.at[slot],
            device_id={"row": peer},
            device_id_type=MESH,
        )

    def put_q(slot_col, peer, sem):
        return pltpu.make_async_remote_copy(
            src_ref=q_ref,
            dst_ref=q_buf.at[pl.ds(slot_col * n_slot, n_slot)],
            send_sem=sem,
            recv_sem=q_recv.at[slot_col],
            device_id={"col": peer},
            device_id_type=MESH,
        )

    order = [0]
    for k in range(1, n_z // 2 + 1):
        order += [k] if 2 * k == n_z else [k, n_z - k]
    put(kv_ref, row, y_sem.at[0], y_peer).start()
    for t in range(1, n_z):
        put(kv_ref, row, z_sem.at[t], z_peers[order[t] - 1]).start()
    put(kv_ref, row, core_sem.at[0], core_peer).start()
    for k, peer in enumerate(col_peers):
        put_q(col, peer, q_send.at[k]).start()
    own_kv.wait()
    own_q.wait()

    def slot_z(t):
        return lax.rem(row - 4 * order[t] + n, n)

    def relay_z(t):
        slot = slot_z(t)
        put(kv_buf.at[slot], slot, y_sem.at[t], y_peer).wait_recv()
        put(kv_buf.at[slot], slot, y_sem.at[t], y_peer).start()
        put(kv_buf.at[slot], slot, core_sem.at[2 * t], core_peer).start()

    def relay_y(t):
        slot = slot_z(t) + 2 - 4 * y
        put(kv_buf.at[slot], slot, core_sem.at[2 * t + 1], core_peer).wait_recv()
        put(kv_buf.at[slot], slot, core_sem.at[2 * t + 1], core_peer).start()

    def bias_group(g, carry):
        pair_copy(g).wait()
        parts = [halves(channel_norm(pair_buf[g, i])) for i in range(group)]
        high = jnp.concatenate([p[0] for p in parts], axis=1)
        low = jnp.concatenate([p[1] for p in parts], axis=1)
        wt_hi = wt_hi_ref[...]
        flat = dot_nt(wt_hi, high) + (dot_nt(wt_hi, low) + dot_nt(wt_lo_ref[...], high))
        bias_buf[:, pl.ds(pl.multiple_of(g * group, group), group), :] = flat.reshape(
            heads, group, flat.shape[1]
        )
        return carry

    for t in range(1, n_z):
        lax.fori_loop(
            (t - 1) * groups // (n_z - 1), t * groups // (n_z - 1), bias_group, 0
        )
        relay_z(t)
        relay_y(t - 1)
    for k in range(1, n_col):
        source = lax.rem(col - k + n_col, n_col)
        put_q(source, col_peers[k - 1], q_send.at[k - 1]).wait_recv()

    scale = F32(head_dim) ** -0.5
    lane = lax.broadcasted_iota(jnp.int32, (rows, wide), 1) // head_dim
    stat_lane = lax.broadcasted_iota(jnp.int32, (rows, stat_ref.shape[2]), 1)
    dot = functools.partial(jnp.dot, preferred_element_type=F32)
    stat_ref[...] = jnp.zeros_like(stat_ref)

    def attend(base):
        part = jnp.zeros((rows, wide), F32)
        for par in range(2):
            slot = base + par
            k_at, v_at = (per, 0) if par == 0 else (0, per)
            q = q_buf[slot]
            kv = kv_buf[slot]
            qs = jnp.concatenate(
                [jnp.where(lane == k_at + m, q, 0.0) for m in range(per)], axis=0
            )
            bias = bias_buf[pl.ds(slot * per, per)].reshape(per * rows, -1)
            scores = dot_nt(qs, kv, HIGH) * scale + bias
            top = jnp.max(scores, axis=1, keepdims=True)
            expo = jnp.exp(scores - top)
            total = jnp.sum(expo, axis=1, keepdims=True)
            e_hi, e_lo = halves(expo)
            v_hi, v_lo = halves(kv)
            out = dot(e_hi, v_hi) + (dot(e_hi, v_lo) + dot(e_lo, v_hi))
            for m in range(per):
                mine = slice(m * rows, (m + 1) * rows)
                part = jnp.where(lane == v_at + m, out[mine], part)
                here = stat_lane == slot * per + m
                stat_ref[0] = jnp.where(here, top[mine], stat_ref[0])
                stat_ref[1] = jnp.where(here, total[mine], stat_ref[1])
        part_ref[lax.div(base, 2)] = part

    for t in range(n_z):
        if t == n_z - 1:
            relay_y(t)

        def chip(u, carry):
            base = slot_z(t) - core + u * (2 - 4 * y)
            slot = base + 1 - core
            put(kv_buf.at[slot], slot, core_sem.at[0], core_peer).wait_recv()
            attend(base)
            return carry

        lax.fori_loop(0, 2, chip, 0)

    for t in range(n_z):
        slot = slot_z(t)
        if t:
            put(kv_ref, slot, z_sem.at[t], y_peer).wait_send()
        put(kv_ref, slot, y_sem.at[t], y_peer).wait_send()
        for u in range(2):
            put(kv_ref, slot, core_sem.at[2 * t + u], core_peer).wait_send()
    for k, peer in enumerate(col_peers):
        put_q(col, peer, q_send.at[k]).wait_send()


def gather_attention(query, key, value, pair, w_bias):
    n, n_col = lax.axis_size("row"), lax.axis_size("col")
    rows, cols, channels = pair.shape
    heads = w_bias.shape[1]
    feats = key.shape[1]
    head_dim = feats * n // heads
    n_slot = query.shape[1] // feats
    group = 8
    eye = jnp.eye(group, dtype=F32)
    wt = (w_bias.T[:, None, None, :] * eye[None, :, :, None]).reshape(
        heads * group, group * channels
    )
    wt_hi, wt_lo = split(wt)
    odd = lax.rem(lax.axis_index("row"), 2) == 1
    kv = jnp.where(
        odd, jnp.concatenate([key, value], axis=1), jnp.concatenate([value, key], axis=1)
    )
    q = query.reshape(rows, n_slot // 2, 2, feats).transpose(1, 2, 0, 3)
    zero = jnp.zeros_like(q[:, 0])
    q = jnp.stack(
        [jnp.concatenate([zero, q[:, 0]], axis=2), jnp.concatenate([q[:, 1], zero], axis=2)],
        axis=1,
    ).reshape(n_slot, rows, 2 * feats)
    any_space = pl.BlockSpec(memory_space=pl.ANY)
    vmem = pl.BlockSpec(memory_space=pltpu.VMEM)
    dma = pltpu.SemaphoreType.DMA
    n_z = n // 4
    return pl.pallas_call(
        functools.partial(gather_attention_kernel, n, n_col, head_dim, heads),
        out_shape=(
            jax.ShapeDtypeStruct((n // 2, rows, 2 * feats), F32),
            jax.ShapeDtypeStruct((2, rows, 128), F32),
        ),
        in_specs=[any_space, any_space, any_space, vmem, vmem],
        out_specs=(vmem, vmem),
        scratch_shapes=[
            pltpu.VMEM((n, cols, 2 * feats), F32),
            pltpu.VMEM((n, rows, 2 * feats), F32),
            pltpu.VMEM((heads, rows, cols), F32),
            pltpu.VMEM((rows // group, group, cols, channels), F32),
            dma((n,)),
            dma((n_z,)),
            dma((n_z,)),
            dma((2 * n_z,)),
            dma((n_col,)),
            dma((n_col,)),
            dma((rows // group,)),
        ],
        compiler_params=pltpu.CompilerParams(
            vmem_limit_bytes=VMEM_LIMIT, collective_id=0, has_side_effects=True
        ),
        name="gather_attention",
    )(kv, q, pair, wt_hi, wt_lo)


def transition_kernel(
    pair_ref, left_ref, right_ref, w_outer_ref, bias_ref, up_ref, down_ref, down_hi_ref, out_ref,
    left_t, right_s, left_d,
):
    step = pl.program_id(0)
    group, cols, channels = pair_ref.shape
    proj = left_ref.shape[1]
    dot = functools.partial(jnp.dot, preferred_element_type=F32)

    @pl.when(step == 0)
    def _():
        left = left_ref[...]
        left_t[...] = left.T
        left_d[...] = jnp.dot(left, w_outer_ref[proj:], precision=HIGH) + bias_ref[...]
        r_hi, r_lo = halves(right_ref[...])
        right_s[...] = jnp.concatenate([r_hi, r_lo, r_hi], axis=1)

    lane = lax.broadcasted_iota(jnp.int32, left_t.shape, 1)
    w_prod = w_outer_ref[:proj]
    w_diff = w_outer_ref[proj:]
    weights = []
    for g in range(group):
        column = jnp.sum(
            jnp.where(lane == step * group + g, left_t[...], 0.0), axis=1, keepdims=True
        )
        w_hi, w_lo = halves(column * w_prod - w_diff)
        weights.append(jnp.concatenate([w_hi, w_hi, w_lo], axis=0))
    outer = dot(right_s[...], jnp.concatenate(weights, axis=1))
    for g in range(group):
        mid = pair_ref[g] + (
            outer[:, g * channels : (g + 1) * channels]
            + left_d[pl.ds(step * group + g, 1), :]
        )
        x_hi, x_lo = halves(channel_norm(mid))
        hidden = jnp.maximum(dot(jnp.concatenate([x_hi, x_lo, x_hi], axis=1), up_ref[...]), 0.0)
        h_hi, h_lo = halves(hidden)
        both = dot(h_hi, down_ref[...])
        out_ref[g] = mid + (
            both[:, :channels] + (both[:, channels:] + dot(h_lo, down_hi_ref[...]))
        )


def transition(pair, left, right, w_outer, outer_bias, w_up, w_down):
    rows, cols, channels = pair.shape
    proj = left.shape[1]
    hidden = w_up.shape[1]
    group = 2
    up_hi, up_lo = split(w_up)
    up = jnp.concatenate([up_hi, up_hi, up_lo], axis=0)
    down_hi, down_lo = split(w_down)
    down = jnp.concatenate([down_hi, down_lo], axis=1)

    def whole(x):
        return pl.BlockSpec(x.shape, lambda i: (0,) * x.ndim)

    block = pl.BlockSpec((group, cols, channels), lambda i: (i, 0, 0))
    fixed = (left, right, w_outer, outer_bias.reshape(1, channels), up, down, down_hi)
    return pl.pallas_call(
        transition_kernel,
        out_shape=jax.ShapeDtypeStruct(pair.shape, F32),
        grid=(rows // group,),
        in_specs=[block] + [whole(x) for x in fixed],
        out_specs=block,
        scratch_shapes=[
            pltpu.VMEM((proj, rows), F32),
            pltpu.VMEM((cols, 3 * proj), BF16),
            pltpu.VMEM((rows, channels), F32),
        ],
        compiler_params=pltpu.CompilerParams(vmem_limit_bytes=VMEM_LIMIT),
        name="transition",
    )(pair, *fixed)


def per_device(
    seq, query, key, value, pair, w_bias, w_out, w_left, w_right, w_outer, outer_bias, w_up, w_down
):
    rows, cols, channels = pair.shape
    heads = w_bias.shape[1]
    width = w_out.shape[0]
    head_dim = width // heads
    proj = w_left.shape[1]
    part, stat = gather_attention(query, key, value, pair, w_bias)
    part = part.transpose(1, 0, 2).reshape(rows, width)
    top, total = stat[0], stat[1]
    every = lax.all_gather(
        jnp.concatenate([part, top[:, :heads], total[:, :heads]], axis=1), "col"
    )
    parts = every[:, :, :width]
    tops = every[:, :, width : width + heads]
    totals = every[:, :, width + heads :]
    scale = jnp.exp(tops - jnp.max(tops, axis=0))
    scale = scale / jnp.sum(scale * totals, axis=0)
    attn = jnp.sum(parts * jnp.repeat(scale, head_dim, axis=2), axis=0)
    seq_new = seq + jnp.dot(attn, w_out, precision=HIGH)
    here = seq.shape[1]
    local_mean = jnp.mean(seq_new, axis=1, keepdims=True)
    centred = seq_new - local_mean
    w_both = jnp.concatenate([w_left, w_right], axis=1)
    projected = jnp.dot(centred, w_both, precision=HIGH)
    spread = jnp.sum(centred * centred, axis=1, keepdims=True)
    column = jnp.broadcast_to(jnp.sum(w_both, axis=0, keepdims=True), (rows, 2 * proj))
    sent = jnp.concatenate([projected, column, local_mean, spread], axis=1)
    every = lax.all_gather(sent, "col")
    means = every[:, :, 4 * proj : 4 * proj + 1]
    spreads = every[:, :, 4 * proj + 1 :]
    mean = jnp.mean(means, axis=0)
    offset = means - mean
    variance = (jnp.sum(spreads, axis=0) + here * jnp.sum(offset * offset, axis=0)) / width
    both = jnp.sum(every[:, :, : 2 * proj] + offset * every[:, :, 2 * proj : 4 * proj], axis=0)
    both = both * lax.rsqrt(variance + 1e-05)
    left = both[:, :proj]
    right_every = lax.all_gather(both[:, proj:], "row", axis=0, tiled=True)
    right = lax.dynamic_slice_in_dim(right_every, lax.axis_index("col") * cols, cols, 0)
    pair_new = transition(pair, left, right, w_outer, outer_bias, w_up, w_down)
    return seq_new, pair_new


def solution(mesh):
    in_specs = (
        P("row", "col"),
        P("row", "col"),
        P("col", "row"),
        P("col", "row"),
        P("row", "col", None),
        P(),
        P(None, "col"),
        P("col", None),
        P("col", None),
        P(),
        P(),
        P(),
        P(),
    )
    out_specs = (P("row", "col"), P("row", "col", None))
    return jax.shard_map(
        per_device, mesh=mesh, in_specs=in_specs, out_specs=out_specs, check_vma=False
    )
```

```python
import functools

import jax
import jax.numpy as jnp
from jax import lax
from jax.experimental import pallas as pl
from jax.experimental.pallas import tpu as pltpu
from jax.sharding import PartitionSpec as P

HIGH = lax.Precision.HIGHEST
F32 = jnp.float32
BF16 = jnp.bfloat16
VMEM_LIMIT = 60 * 1024 * 1024
MESH = pl.DeviceIdType.MESH


def halves(x):
    high = x.astype(BF16)
    low = (x - high.astype(F32)).astype(BF16)
    return high, low


def split(x):
    kept = lax.reduce_precision(x, 8, 7)
    return kept.astype(BF16), (x - kept).astype(BF16)


def channel_norm(x):
    centre = x - jnp.mean(x, axis=-1, keepdims=True)
    return centre * lax.rsqrt(jnp.mean(centre * centre, axis=-1, keepdims=True) + 1e-05)


def dot_nt(a, b, precision=None):
    return lax.dot_general(
        a, b, (((1,), (1,)), ((), ())), precision=precision, preferred_element_type=F32
    )


def gather_attention_kernel(
    n, n_col, head_dim, heads,
    kv_ref, q_ref, pair_ref, wt_hi_ref, wt_lo_ref,
    part_ref, stat_ref,
    kv_buf, q_buf, bias_buf, pair_buf,
    recv_sem, z_sem, y_sem, core_sem, q_send, q_recv, pair_sem,
):
    n_z = n // 4
    n_slot, rows, wide = q_ref.shape
    groups, group = pair_buf.shape[:2]
    per = wide // 2 // head_dim
    row, col = lax.axis_index("row"), lax.axis_index("col")
    core, y = lax.rem(row, 2), lax.rem(lax.div(row, 2), 2)
    core_peer, y_peer = row + 1 - 2 * core, row + 2 - 4 * y
    z_peers = [lax.rem(row + 4 * k, n) for k in range(1, n_z)]
    col_peers = [lax.rem(col + k, n_col) for k in range(1, n_col)]

    def pair_copy(g):
        return pltpu.make_async_copy(
            pair_ref.at[pl.ds(g * group, group)], pair_buf.at[g], pair_sem.at[g]
        )

    for g in range(groups):
        pair_copy(g).start()
    own_kv = pltpu.make_async_copy(kv_ref, kv_buf.at[row], recv_sem.at[row])
    own_kv.start()
    own_q = pltpu.make_async_copy(
        q_ref, q_buf.at[pl.ds(col * n_slot, n_slot)], q_recv.at[col]
    )
    own_q.start()

    barrier = pltpu.get_barrier_semaphore()
    for peer in z_peers + [y_peer, core_peer]:
        pl.semaphore_signal(barrier, inc=1, device_id={"row": peer}, device_id_type=MESH)
    for peer in col_peers:
        pl.semaphore_signal(barrier, inc=1, device_id={"col": peer}, device_id_type=MESH)
    pl.semaphore_wait(barrier, n_z + n_col)

    def put(src, slot, sem, peer):
        return pltpu.make_async_remote_copy(
            src_ref=src,
            dst_ref=kv_buf.at[slot],
            send_sem=sem,
            recv_sem=recv_sem.at[slot],
            device_id={"row": peer},
            device_id_type=MESH,
        )

    def put_q(slot_col, peer, sem):
        return pltpu.make_async_remote_copy(
            src_ref=q_ref,
            dst_ref=q_buf.at[pl.ds(slot_col * n_slot, n_slot)],
            send_sem=sem,
            recv_sem=q_recv.at[slot_col],
            device_id={"col": peer},
            device_id_type=MESH,
        )

    order = [0]
    for k in range(1, n_z // 2 + 1):
        order += [k] if 2 * k == n_z else [k, n_z - k]
    put(kv_ref, row, y_sem.at[0], y_peer).start()
    for t in range(1, n_z):
        put(kv_ref, row, z_sem.at[t], z_peers[order[t] - 1]).start()
    put(kv_ref, row, core_sem.at[0], core_peer).start()
    for k, peer in enumerate(col_peers):
        put_q(col, peer, q_send.at[k]).start()
    own_kv.wait()
    own_q.wait()

    def slot_z(t):
        return lax.rem(row - 4 * order[t] + n, n)

    def relay_z(t):
        slot = slot_z(t)
        put(kv_buf.at[slot], slot, y_sem.at[t], y_peer).wait_recv()
        put(kv_buf.at[slot], slot, y_sem.at[t], y_peer).start()
        put(kv_buf.at[slot], slot, core_sem.at[2 * t], core_peer).start()

    def relay_y(t):
        slot = slot_z(t) + 2 - 4 * y
        put(kv_buf.at[slot], slot, core_sem.at[2 * t + 1], core_peer).wait_recv()
        put(kv_buf.at[slot], slot, core_sem.at[2 * t + 1], core_peer).start()

    def bias_group(g, carry):
        pair_copy(g).wait()
        parts = [halves(channel_norm(pair_buf[g, i])) for i in range(group)]
        high = jnp.concatenate([p[0] for p in parts], axis=1)
        low = jnp.concatenate([p[1] for p in parts], axis=1)
        wt_hi = wt_hi_ref[...]
        flat = dot_nt(wt_hi, high) + (dot_nt(wt_hi, low) + dot_nt(wt_lo_ref[...], high))
        bias_buf[:, pl.ds(pl.multiple_of(g * group, group), group), :] = flat.reshape(
            heads, group, flat.shape[1]
        )
        return carry

    for t in range(1, n_z):
        lax.fori_loop(
            (t - 1) * groups // (n_z - 1), t * groups // (n_z - 1), bias_group, 0
        )
        relay_z(t)
        relay_y(t - 1)
    for k in range(1, n_col):
        source = lax.rem(col - k + n_col, n_col)
        put_q(source, col_peers[k - 1], q_send.at[k - 1]).wait_recv()

    scale = F32(head_dim) ** -0.5
    lane = lax.broadcasted_iota(jnp.int32, (rows, wide), 1) // head_dim
    stat_lane = lax.broadcasted_iota(jnp.int32, (rows, stat_ref.shape[2]), 1)
    dot = functools.partial(jnp.dot, preferred_element_type=F32)
    stat_ref[...] = jnp.zeros_like(stat_ref)

    def attend(base):
        part = jnp.zeros((rows, wide), F32)
        for par in range(2):
            slot = base + par
            k_at, v_at = (per, 0) if par == 0 else (0, per)
            q = q_buf[slot]
            kv = kv_buf[slot]
            qs = jnp.concatenate(
                [jnp.where(lane == k_at + m, q, 0.0) for m in range(per)], axis=0
            )
            bias = bias_buf[pl.ds(slot * per, per)].reshape(per * rows, -1)
            scores = dot_nt(qs, kv, HIGH) * scale + bias
            top = jnp.max(scores, axis=1, keepdims=True)
            expo = jnp.exp(scores - top)
            total = jnp.sum(expo, axis=1, keepdims=True)
            e_hi, e_lo = halves(expo)
            v_hi, v_lo = halves(kv)
            out = dot(e_hi, v_hi) + (dot(e_hi, v_lo) + dot(e_lo, v_hi))
            for m in range(per):
                mine = slice(m * rows, (m + 1) * rows)
                part = jnp.where(lane == v_at + m, out[mine], part)
                here = stat_lane == slot * per + m
                stat_ref[0] = jnp.where(here, top[mine], stat_ref[0])
                stat_ref[1] = jnp.where(here, total[mine], stat_ref[1])
        part_ref[lax.div(base, 2)] = part

    for t in range(n_z):
        if t == n_z - 1:
            relay_y(t)

        def chip(u, carry):
            base = slot_z(t) - core + u * (2 - 4 * y)
            slot = base + 1 - core
            put(kv_buf.at[slot], slot, core_sem.at[0], core_peer).wait_recv()
            attend(base)
            return carry

        lax.fori_loop(0, 2, chip, 0)

    for t in range(n_z):
        slot = slot_z(t)
        if t:
            put(kv_ref, slot, z_sem.at[t], y_peer).wait_send()
        put(kv_ref, slot, y_sem.at[t], y_peer).wait_send()
        for u in range(2):
            put(kv_ref, slot, core_sem.at[2 * t + u], core_peer).wait_send()
    for k, peer in enumerate(col_peers):
        put_q(col, peer, q_send.at[k]).wait_send()


def gather_attention(query, key, value, pair, w_bias):
    n, n_col = lax.axis_size("row"), lax.axis_size("col")
    rows, cols, channels = pair.shape
    heads = w_bias.shape[1]
    feats = key.shape[1]
    head_dim = feats * n // heads
    n_slot = query.shape[1] // feats
    group = 8
    eye = jnp.eye(group, dtype=F32)
    wt = (w_bias.T[:, None, None, :] * eye[None, :, :, None]).reshape(
        heads * group, group * channels
    )
    wt_hi, wt_lo = split(wt)
    odd = lax.rem(lax.axis_index("row"), 2) == 1
    kv = jnp.where(
        odd, jnp.concatenate([key, value], axis=1), jnp.concatenate([value, key], axis=1)
    )
    q = query.reshape(rows, n_slot // 2, 2, feats).transpose(1, 2, 0, 3)
    zero = jnp.zeros_like(q[:, 0])
    q = jnp.stack(
        [jnp.concatenate([zero, q[:, 0]], axis=2), jnp.concatenate([q[:, 1], zero], axis=2)],
        axis=1,
    ).reshape(n_slot, rows, 2 * feats)
    any_space = pl.BlockSpec(memory_space=pl.ANY)
    vmem = pl.BlockSpec(memory_space=pltpu.VMEM)
    dma = pltpu.SemaphoreType.DMA
    n_z = n // 4
    return pl.pallas_call(
        functools.partial(gather_attention_kernel, n, n_col, head_dim, heads),
        out_shape=(
            jax.ShapeDtypeStruct((n // 2, rows, 2 * feats), F32),
            jax.ShapeDtypeStruct((2, rows, 128), F32),
        ),
        in_specs=[any_space, any_space, any_space, vmem, vmem],
        out_specs=(vmem, vmem),
        scratch_shapes=[
            pltpu.VMEM((n, cols, 2 * feats), F32),
            pltpu.VMEM((n, rows, 2 * feats), F32),
            pltpu.VMEM((heads, rows, cols), F32),
            pltpu.VMEM((rows // group, group, cols, channels), F32),
            dma((n,)),
            dma((n_z,)),
            dma((n_z,)),
            dma((2 * n_z,)),
            dma((n_col,)),
            dma((n_col,)),
            dma((rows // group,)),
        ],
        compiler_params=pltpu.CompilerParams(
            vmem_limit_bytes=VMEM_LIMIT, collective_id=0, has_side_effects=True
        ),
        name="gather_attention",
    )(kv, q, pair, wt_hi, wt_lo)


def merge_kernel(
    n, n_col, head_dim, heads,
    part_ref, stat_ref, seq_ref, w_out_ref, w_both_ref,
    seq_out, left_out, right_out,
    part_buf, stat_buf, packet, packet_buf, both_buf, right_buf,
    part_send, part_recv, stat_send, stat_recv, pack_send, pack_recv,
    right_send, right_recv, relay_send,
):
    rows, here = seq_ref.shape
    width = w_out_ref.shape[0]
    proj = left_out.shape[1]
    blocks = right_buf.shape[0]
    row, col = lax.axis_index("row"), lax.axis_index("col")
    core = lax.rem(row, 2)
    core_peer = row + 1 - 2 * core
    col_peers = [lax.rem(col + k, n_col) for k in range(1, n_col)]
    row_peers = [lax.rem(row + 2 * k, n) for k in range(1, n // 2)]

    barrier = pltpu.get_barrier_semaphore()
    for peer in row_peers + [core_peer]:
        pl.semaphore_signal(barrier, inc=1, device_id={"row": peer}, device_id_type=MESH)
    for peer in col_peers:
        pl.semaphore_signal(barrier, inc=1, device_id={"col": peer}, device_id_type=MESH)
    pl.semaphore_wait(barrier, n // 2 + n_col - 1)

    def put(src, dst, send, recv, peer):
        return pltpu.make_async_remote_copy(
            src_ref=src, dst_ref=dst, send_sem=send, recv_sem=recv,
            device_id=peer, device_id_type=MESH,
        )

    def over_col(src, buf, send, recv):
        return [
            put(src, buf.at[k], send.at[k], recv.at[k], {"col": peer})
            for k, peer in enumerate(col_peers)
        ]

    stats = over_col(stat_ref, stat_buf, stat_send, stat_recv)
    parts = over_col(part_ref, part_buf, part_send, part_recv)
    for copy in stats + parts:
        copy.start()
    for copy in stats:
        copy.wait()
    tops = [stat_ref[0]] + [stat_buf[k, 0] for k in range(n_col - 1)]
    totals = [stat_ref[1]] + [stat_buf[k, 1] for k in range(n_col - 1)]
    highest = functools.reduce(jnp.maximum, tops)
    scales = [jnp.exp(top - highest) for top in tops]
    total = sum(scale * t for scale, t in zip(scales, totals))
    lane = lax.broadcasted_iota(jnp.int32, total.shape, 1)
    total = jnp.where(lane < heads, total, 1.0)
    spread_of = (
        lax.broadcasted_iota(jnp.int32, (total.shape[1], width), 0)
        == lax.broadcasted_iota(jnp.int32, (total.shape[1], width), 1) // head_dim
    ).astype(F32)
    weights = [
        jnp.dot(scale / total, spread_of, precision=HIGH, preferred_element_type=F32)
        for scale in scales
    ]
    for copy in parts:
        copy.wait()

    def dense(load):
        return jnp.concatenate([load(m) for m in range(part_ref.shape[0])], axis=1)

    attn = dense(lambda m: part_ref[m]) * weights[0]
    for k in range(n_col - 1):
        attn = attn + dense(lambda m: part_buf[k, m]) * weights[k + 1]
    seq_new = seq_ref[...] + jnp.dot(
        attn, w_out_ref[...], precision=HIGH, preferred_element_type=F32
    )
    seq_out[...] = seq_new

    local_mean = jnp.mean(seq_new, axis=1, keepdims=True)
    centred = seq_new - local_mean
    spread = jnp.sum(centred * centred, axis=1, keepdims=True)
    w_both = w_both_ref[...]
    packet[:rows] = jnp.dot(centred, w_both, precision=HIGH, preferred_element_type=F32)
    lane = lax.broadcasted_iota(jnp.int32, (rows, 2 * proj), 1)
    packet[rows : 2 * rows] = jnp.where(lane < proj, local_mean, spread)
    packet[2 * rows :] = jnp.broadcast_to(
        jnp.sum(w_both, axis=0, keepdims=True), (8, 2 * proj)
    )
    packets = over_col(packet, packet_buf, pack_send, pack_recv)
    for copy in packets:
        copy.start()
    for copy in packets:
        copy.wait()
    every = [packet[...]] + [packet_buf[k] for k in range(n_col - 1)]
    means = [p[rows : 2 * rows, :1] for p in every]
    mean = sum(means) / n_col
    offsets = [m - mean for m in means]
    variance = (
        sum(p[rows : 2 * rows, proj : proj + 1] for p in every)
        + here * sum(o * o for o in offsets)
    ) / width
    both = sum(p[:rows] + o * p[2 * rows : 2 * rows + 1] for p, o in zip(every, offsets))
    both = both * lax.rsqrt(variance + 1e-05)
    left_out[...] = both[:, :proj]
    both_buf[...] = both

    mine = lax.div(row, blocks) == col
    own = lax.rem(row, blocks)

    def row_copies():
        return [
            put(both_buf, right_buf.at[own], right_send.at[k], right_recv.at[own], {"row": peer})
            for k, peer in enumerate(row_peers)
        ]

    @pl.when(mine)
    def _():
        for copy in row_copies():
            copy.start()
        keep = pltpu.make_async_copy(both_buf, right_buf.at[own], right_recv.at[own])
        keep.start()
        keep.wait()

    def relay(j, block):
        slot = right_buf.at[block]
        return put(slot, slot, relay_send.at[j], right_recv.at[block], {"row": core_peer})

    for j in range(blocks // 2):
        block = 2 * j + core

        @pl.when(col * blocks + block != row)
        def _():
            relay(j, block).wait_recv()

        relay(j, block).start()
    for j in range(blocks // 2):
        relay(j, 2 * j + 1 - core).wait_recv()
    for b in range(blocks):
        right_out[b * rows : (b + 1) * rows] = right_buf[b][:, proj:]
    for j in range(blocks // 2):
        relay(j, 2 * j + core).wait_send()

    @pl.when(mine)
    def _():
        for copy in row_copies():
            copy.wait_send()


def merge(part, stat, seq, w_out, w_left, w_right, head_dim, heads, cols):
    n, n_col = lax.axis_size("row"), lax.axis_size("col")
    rows = seq.shape[0]
    proj = w_left.shape[1]
    blocks = cols // rows
    w_both = jnp.concatenate([w_left, w_right], axis=1)
    vmem = pl.BlockSpec(memory_space=pltpu.VMEM)
    dma = pltpu.SemaphoreType.DMA
    peers = n_col - 1
    return pl.pallas_call(
        functools.partial(merge_kernel, n, n_col, head_dim, heads),
        out_shape=(
            jax.ShapeDtypeStruct(seq.shape, F32),
            jax.ShapeDtypeStruct((rows, proj), F32),
            jax.ShapeDtypeStruct((cols, proj), F32),
        ),
        in_specs=[vmem] * 5,
        out_specs=(vmem,) * 3,
        scratch_shapes=[
            pltpu.VMEM((peers, *part.shape), F32),
            pltpu.VMEM((peers, *stat.shape), F32),
            pltpu.VMEM((2 * rows + 8, 2 * proj), F32),
            pltpu.VMEM((peers, 2 * rows + 8, 2 * proj), F32),
            pltpu.VMEM((rows, 2 * proj), F32),
            pltpu.VMEM((blocks, rows, 2 * proj), F32),
            dma((peers,)), dma((peers,)), dma((peers,)), dma((peers,)), dma((peers,)),
            dma((peers,)), dma((n // 2 - 1,)), dma((blocks,)), dma((blocks // 2,)),
        ],
        compiler_params=pltpu.CompilerParams(
            vmem_limit_bytes=VMEM_LIMIT, collective_id=1, has_side_effects=True
        ),
        name="merge",
    )(part, stat, seq, w_out, w_both)


def transition_kernel(
    pair_ref, left_ref, right_ref, w_outer_ref, bias_ref, up_ref, down_ref, down_hi_ref, out_ref,
    left_t, right_s, left_d,
):
    step = pl.program_id(0)
    group, cols, channels = pair_ref.shape
    proj = left_ref.shape[1]
    dot = functools.partial(jnp.dot, preferred_element_type=F32)

    @pl.when(step == 0)
    def _():
        left = left_ref[...]
        left_t[...] = left.T
        left_d[...] = jnp.dot(left, w_outer_ref[proj:], precision=HIGH) + bias_ref[...]
        r_hi, r_lo = halves(right_ref[...])
        right_s[...] = jnp.concatenate([r_hi, r_lo, r_hi], axis=1)

    lane = lax.broadcasted_iota(jnp.int32, left_t.shape, 1)
    w_prod = w_outer_ref[:proj]
    w_diff = w_outer_ref[proj:]
    weights = []
    for g in range(group):
        column = jnp.sum(
            jnp.where(lane == step * group + g, left_t[...], 0.0), axis=1, keepdims=True
        )
        w_hi, w_lo = halves(column * w_prod - w_diff)
        weights.append(jnp.concatenate([w_hi, w_hi, w_lo], axis=0))
    outer = dot(right_s[...], jnp.concatenate(weights, axis=1))
    for g in range(group):
        mid = pair_ref[g] + (
            outer[:, g * channels : (g + 1) * channels]
            + left_d[pl.ds(step * group + g, 1), :]
        )
        x_hi, x_lo = halves(channel_norm(mid))
        hidden = jnp.maximum(dot(jnp.concatenate([x_hi, x_lo, x_hi], axis=1), up_ref[...]), 0.0)
        h_hi, h_lo = halves(hidden)
        both = dot(h_hi, down_ref[...])
        out_ref[g] = mid + (
            both[:, :channels] + (both[:, channels:] + dot(h_lo, down_hi_ref[...]))
        )


def transition(pair, left, right, w_outer, outer_bias, w_up, w_down):
    rows, cols, channels = pair.shape
    proj = left.shape[1]
    hidden = w_up.shape[1]
    group = 2
    up_hi, up_lo = split(w_up)
    up = jnp.concatenate([up_hi, up_hi, up_lo], axis=0)
    down_hi, down_lo = split(w_down)
    down = jnp.concatenate([down_hi, down_lo], axis=1)

    def whole(x):
        return pl.BlockSpec(x.shape, lambda i: (0,) * x.ndim)

    block = pl.BlockSpec((group, cols, channels), lambda i: (i, 0, 0))
    fixed = (left, right, w_outer, outer_bias.reshape(1, channels), up, down, down_hi)
    return pl.pallas_call(
        transition_kernel,
        out_shape=jax.ShapeDtypeStruct(pair.shape, F32),
        grid=(rows // group,),
        in_specs=[block] + [whole(x) for x in fixed],
        out_specs=block,
        scratch_shapes=[
            pltpu.VMEM((proj, rows), F32),
            pltpu.VMEM((cols, 3 * proj), BF16),
            pltpu.VMEM((rows, channels), F32),
        ],
        compiler_params=pltpu.CompilerParams(vmem_limit_bytes=VMEM_LIMIT),
        name="transition",
    )(pair, *fixed)


def per_device(
    seq, query, key, value, pair, w_bias, w_out, w_left, w_right, w_outer, outer_bias, w_up, w_down
):
    rows, cols, channels = pair.shape
    heads = w_bias.shape[1]
    width = w_out.shape[0]
    head_dim = width // heads
    part, stat = gather_attention(query, key, value, pair, w_bias)
    seq_new, left, right = merge(
        part, stat, seq, w_out, w_left, w_right, head_dim, heads, cols
    )
    pair_new = transition(pair, left, right, w_outer, outer_bias, w_up, w_down)
    return seq_new, pair_new


def solution(mesh):
    in_specs = (
        P("row", "col"),
        P("row", "col"),
        P("col", "row"),
        P("col", "row"),
        P("row", "col", None),
        P(),
        P(None, "col"),
        P("col", None),
        P("col", None),
        P(),
        P(),
        P(),
        P(),
    )
    out_specs = (P("row", "col"), P("row", "col", None))
    return jax.shard_map(
        per_device, mesh=mesh, in_specs=in_specs, out_specs=out_specs, check_vma=False
    )
```

```python
import functools

import jax
import jax.numpy as jnp
from jax import lax
from jax.experimental import pallas as pl
from jax.experimental.pallas import tpu as pltpu
from jax.sharding import PartitionSpec as P

HIGH = lax.Precision.HIGHEST
F32 = jnp.float32
BF16 = jnp.bfloat16
VMEM_LIMIT = 60 * 1024 * 1024
MESH = pl.DeviceIdType.MESH


def halves(x):
    high = x.astype(BF16)
    low = (x - high.astype(F32)).astype(BF16)
    return high, low


def split(x):
    kept = lax.reduce_precision(x, 8, 7)
    return kept.astype(BF16), (x - kept).astype(BF16)


def channel_norm(x):
    centre = x - jnp.mean(x, axis=-1, keepdims=True)
    return centre * lax.rsqrt(jnp.mean(centre * centre, axis=-1, keepdims=True) + 1e-05)


def dot_nt(a, b, precision=None):
    return lax.dot_general(
        a, b, (((1,), (1,)), ((), ())), precision=precision, preferred_element_type=F32
    )


def gather_attention_kernel(
    n, n_col, head_dim, heads,
    kv_ref, q_ref, pair_ref, wt_hi_ref, wt_lo_ref,
    part_ref, stat_ref,
    kv_buf, q_buf, bias_buf, pair_buf,
    recv_sem, z_sem, y_sem, core_sem, q_send, q_recv, pair_sem,
):
    n_z = n // 4
    n_slot, rows, wide = q_ref.shape
    groups, group = pair_buf.shape[:2]
    per = wide // 2 // head_dim
    row, col = lax.axis_index("row"), lax.axis_index("col")
    core, y = lax.rem(row, 2), lax.rem(lax.div(row, 2), 2)
    core_peer, y_peer = row + 1 - 2 * core, row + 2 - 4 * y
    z_peers = [lax.rem(row + 4 * k, n) for k in range(1, n_z)]
    col_peers = [lax.rem(col + k, n_col) for k in range(1, n_col)]

    def pair_copy(g):
        return pltpu.make_async_copy(
            pair_ref.at[pl.ds(g * group, group)], pair_buf.at[g], pair_sem.at[g]
        )

    for g in range(groups):
        pair_copy(g).start()
    own_kv = pltpu.make_async_copy(kv_ref, kv_buf.at[row], recv_sem.at[row])
    own_kv.start()
    own_q = pltpu.make_async_copy(
        q_ref, q_buf.at[pl.ds(col * n_slot, n_slot)], q_recv.at[col]
    )
    own_q.start()

    barrier = pltpu.get_barrier_semaphore()
    for peer in z_peers + [y_peer, core_peer]:
        pl.semaphore_signal(barrier, inc=1, device_id={"row": peer}, device_id_type=MESH)
    for peer in col_peers:
        pl.semaphore_signal(barrier, inc=1, device_id={"col": peer}, device_id_type=MESH)
    pl.semaphore_wait(barrier, n_z + n_col)

    def put(src, slot, sem, peer):
        return pltpu.make_async_remote_copy(
            src_ref=src,
            dst_ref=kv_buf.at[slot],
            send_sem=sem,
            recv_sem=recv_sem.at[slot],
            device_id={"row": peer},
            device_id_type=MESH,
        )

    def put_q(slot_col, peer, sem):
        return pltpu.make_async_remote_copy(
            src_ref=q_ref,
            dst_ref=q_buf.at[pl.ds(slot_col * n_slot, n_slot)],
            send_sem=sem,
            recv_sem=q_recv.at[slot_col],
            device_id={"col": peer},
            device_id_type=MESH,
        )

    order = [0]
    for k in range(1, n_z // 2 + 1):
        order += [k] if 2 * k == n_z else [k, n_z - k]
    put(kv_ref, row, y_sem.at[0], y_peer).start()
    for t in range(1, n_z):
        put(kv_ref, row, z_sem.at[t], z_peers[order[t] - 1]).start()
    put(kv_ref, row, core_sem.at[0], core_peer).start()
    for k, peer in enumerate(col_peers):
        put_q(col, peer, q_send.at[k]).start()
    own_kv.wait()
    own_q.wait()

    def slot_z(t):
        return lax.rem(row - 4 * order[t] + n, n)

    def relay_z(t):
        slot = slot_z(t)
        put(kv_buf.at[slot], slot, y_sem.at[t], y_peer).wait_recv()
        put(kv_buf.at[slot], slot, y_sem.at[t], y_peer).start()
        put(kv_buf.at[slot], slot, core_sem.at[2 * t], core_peer).start()

    def relay_y(t):
        slot = slot_z(t) + 2 - 4 * y
        put(kv_buf.at[slot], slot, core_sem.at[2 * t + 1], core_peer).wait_recv()
        put(kv_buf.at[slot], slot, core_sem.at[2 * t + 1], core_peer).start()

    def bias_group(g, carry):
        pair_copy(g).wait()
        parts = [halves(channel_norm(pair_buf[g, i])) for i in range(group)]
        high = jnp.concatenate([p[0] for p in parts], axis=1)
        low = jnp.concatenate([p[1] for p in parts], axis=1)
        wt_hi = wt_hi_ref[...]
        flat = dot_nt(wt_hi, high) + (dot_nt(wt_hi, low) + dot_nt(wt_lo_ref[...], high))
        bias_buf[:, pl.ds(pl.multiple_of(g * group, group), group), :] = flat.reshape(
            heads, group, flat.shape[1]
        )
        return carry

    for t in range(1, n_z):
        lax.fori_loop(
            (t - 1) * groups // (n_z - 1), t * groups // (n_z - 1), bias_group, 0
        )
        relay_z(t)
        relay_y(t - 1)
    for k in range(1, n_col):
        source = lax.rem(col - k + n_col, n_col)
        put_q(source, col_peers[k - 1], q_send.at[k - 1]).wait_recv()

    scale = F32(head_dim) ** -0.5
    lane = lax.broadcasted_iota(jnp.int32, (rows, wide), 1) // head_dim
    stat_lane = lax.broadcasted_iota(jnp.int32, (rows, stat_ref.shape[2]), 1)
    dot = functools.partial(jnp.dot, preferred_element_type=F32)
    stat_ref[...] = jnp.zeros_like(stat_ref)

    def attend(base):
        part = jnp.zeros((rows, wide), F32)
        for par in range(2):
            slot = base + par
            k_at, v_at = (per, 0) if par == 0 else (0, per)
            q = q_buf[slot]
            kv = kv_buf[slot]
            qs = jnp.concatenate(
                [jnp.where(lane == k_at + m, q, 0.0) for m in range(per)], axis=0
            )
            bias = bias_buf[pl.ds(slot * per, per)].reshape(per * rows, -1)
            scores = dot_nt(qs, kv, HIGH) * scale + bias
            top = jnp.max(scores, axis=1, keepdims=True)
            expo = jnp.exp(scores - top)
            total = jnp.sum(expo, axis=1, keepdims=True)
            e_hi, e_lo = halves(expo)
            v_hi, v_lo = halves(kv)
            out = dot(e_hi, v_hi) + (dot(e_hi, v_lo) + dot(e_lo, v_hi))
            for m in range(per):
                mine = slice(m * rows, (m + 1) * rows)
                part = jnp.where(lane == v_at + m, out[mine], part)
                here = stat_lane == slot * per + m
                stat_ref[0] = jnp.where(here, top[mine], stat_ref[0])
                stat_ref[1] = jnp.where(here, total[mine], stat_ref[1])
        part_ref[lax.div(base, 2)] = part

    for t in range(n_z):
        if t == n_z - 1:
            relay_y(t)

        def chip(u, carry):
            base = slot_z(t) - core + u * (2 - 4 * y)
            slot = base + 1 - core
            put(kv_buf.at[slot], slot, core_sem.at[0], core_peer).wait_recv()
            attend(base)
            return carry

        lax.fori_loop(0, 2, chip, 0)

    for t in range(n_z):
        slot = slot_z(t)
        if t:
            put(kv_ref, slot, z_sem.at[t], y_peer).wait_send()
        put(kv_ref, slot, y_sem.at[t], y_peer).wait_send()
        for u in range(2):
            put(kv_ref, slot, core_sem.at[2 * t + u], core_peer).wait_send()
    for k, peer in enumerate(col_peers):
        put_q(col, peer, q_send.at[k]).wait_send()


def gather_attention(query, key, value, pair, w_bias):
    n, n_col = lax.axis_size("row"), lax.axis_size("col")
    rows, cols, channels = pair.shape
    heads = w_bias.shape[1]
    feats = key.shape[1]
    head_dim = feats * n // heads
    n_slot = query.shape[1] // feats
    group = 8
    eye = jnp.eye(group, dtype=F32)
    wt = (w_bias.T[:, None, None, :] * eye[None, :, :, None]).reshape(
        heads * group, group * channels
    )
    wt_hi, wt_lo = split(wt)
    odd = lax.rem(lax.axis_index("row"), 2) == 1
    kv = jnp.where(
        odd, jnp.concatenate([key, value], axis=1), jnp.concatenate([value, key], axis=1)
    )
    q = query.reshape(rows, n_slot // 2, 2, feats).transpose(1, 2, 0, 3)
    zero = jnp.zeros_like(q[:, 0])
    q = jnp.stack(
        [jnp.concatenate([zero, q[:, 0]], axis=2), jnp.concatenate([q[:, 1], zero], axis=2)],
        axis=1,
    ).reshape(n_slot, rows, 2 * feats)
    any_space = pl.BlockSpec(memory_space=pl.ANY)
    vmem = pl.BlockSpec(memory_space=pltpu.VMEM)
    dma = pltpu.SemaphoreType.DMA
    n_z = n // 4
    return pl.pallas_call(
        functools.partial(gather_attention_kernel, n, n_col, head_dim, heads),
        out_shape=(
            jax.ShapeDtypeStruct((n // 2, rows, 2 * feats), F32),
            jax.ShapeDtypeStruct((2, rows, 128), F32),
        ),
        in_specs=[any_space, any_space, any_space, vmem, vmem],
        out_specs=(vmem, vmem),
        scratch_shapes=[
            pltpu.VMEM((n, cols, 2 * feats), F32),
            pltpu.VMEM((n, rows, 2 * feats), F32),
            pltpu.VMEM((heads, rows, cols), F32),
            pltpu.VMEM((rows // group, group, cols, channels), F32),
            dma((n,)),
            dma((n_z,)),
            dma((n_z,)),
            dma((2 * n_z,)),
            dma((n_col,)),
            dma((n_col,)),
            dma((rows // group,)),
        ],
        compiler_params=pltpu.CompilerParams(
            vmem_limit_bytes=VMEM_LIMIT, collective_id=0, has_side_effects=True
        ),
        name="gather_attention",
    )(kv, q, pair, wt_hi, wt_lo)


def merge_kernel(
    n, n_col, head_dim, heads,
    part_ref, stat_ref, seq_ref, w_out_ref, w_both_ref,
    seq_out, left_out, right_out,
    part_buf, stat_buf, packet, packet_buf, both_buf, right_buf,
    part_send, part_recv, stat_send, stat_recv, pack_send, pack_recv,
    right_send, right_recv, relay_send,
):
    rows, here = seq_ref.shape
    width = w_out_ref.shape[0]
    proj = left_out.shape[1]
    blocks = right_buf.shape[0]
    row, col = lax.axis_index("row"), lax.axis_index("col")
    core = lax.rem(row, 2)
    core_peer = row + 1 - 2 * core
    col_peers = [lax.rem(col + k, n_col) for k in range(1, n_col)]
    row_peers = [lax.rem(row + 2 * k, n) for k in range(1, n // 2)]

    barrier = pltpu.get_barrier_semaphore()
    for peer in row_peers + [core_peer]:
        pl.semaphore_signal(barrier, inc=1, device_id={"row": peer}, device_id_type=MESH)
    for peer in col_peers:
        pl.semaphore_signal(barrier, inc=1, device_id={"col": peer}, device_id_type=MESH)
    pl.semaphore_wait(barrier, n // 2 + n_col - 1)

    def put(src, dst, send, recv, peer):
        return pltpu.make_async_remote_copy(
            src_ref=src, dst_ref=dst, send_sem=send, recv_sem=recv,
            device_id=peer, device_id_type=MESH,
        )

    def over_col(src, buf, send, recv):
        return [
            put(src, buf.at[k], send.at[k], recv.at[k], {"col": peer})
            for k, peer in enumerate(col_peers)
        ]

    stats = over_col(stat_ref, stat_buf, stat_send, stat_recv)
    parts = over_col(part_ref, part_buf, part_send, part_recv)
    for copy in stats + parts:
        copy.start()
    for copy in stats:
        copy.wait()
    tops = [stat_ref[0]] + [stat_buf[k, 0] for k in range(n_col - 1)]
    totals = [stat_ref[1]] + [stat_buf[k, 1] for k in range(n_col - 1)]
    highest = functools.reduce(jnp.maximum, tops)
    scales = [jnp.exp(top - highest) for top in tops]
    total = sum(scale * t for scale, t in zip(scales, totals))
    lane = lax.broadcasted_iota(jnp.int32, total.shape, 1)
    total = jnp.where(lane < heads, total, 1.0)
    spread_of = (
        lax.broadcasted_iota(jnp.int32, (total.shape[1], width), 0)
        == lax.broadcasted_iota(jnp.int32, (total.shape[1], width), 1) // head_dim
    ).astype(F32)
    weights = [
        jnp.dot(scale / total, spread_of, precision=HIGH, preferred_element_type=F32)
        for scale in scales
    ]
    for copy in parts:
        copy.wait()

    def dense(load):
        return jnp.concatenate([load(m) for m in range(part_ref.shape[0])], axis=1)

    attn = dense(lambda m: part_ref[m]) * weights[0]
    for k in range(n_col - 1):
        attn = attn + dense(lambda m: part_buf[k, m]) * weights[k + 1]
    seq_new = seq_ref[...] + jnp.dot(
        attn, w_out_ref[...], precision=HIGH, preferred_element_type=F32
    )
    seq_out[...] = seq_new

    local_mean = jnp.mean(seq_new, axis=1, keepdims=True)
    centred = seq_new - local_mean
    spread = jnp.sum(centred * centred, axis=1, keepdims=True)
    w_both = w_both_ref[...]
    packet[:rows] = jnp.dot(centred, w_both, precision=HIGH, preferred_element_type=F32)
    lane = lax.broadcasted_iota(jnp.int32, (rows, 2 * proj), 1)
    packet[rows : 2 * rows] = jnp.where(lane < proj, local_mean, spread)
    packet[2 * rows :] = jnp.broadcast_to(
        jnp.sum(w_both, axis=0, keepdims=True), (8, 2 * proj)
    )
    packets = over_col(packet, packet_buf, pack_send, pack_recv)
    for copy in packets:
        copy.start()
    for copy in packets:
        copy.wait()
    every = [packet[...]] + [packet_buf[k] for k in range(n_col - 1)]
    means = [p[rows : 2 * rows, :1] for p in every]
    mean = sum(means) / n_col
    offsets = [m - mean for m in means]
    variance = (
        sum(p[rows : 2 * rows, proj : proj + 1] for p in every)
        + here * sum(o * o for o in offsets)
    ) / width
    both = sum(p[:rows] + o * p[2 * rows : 2 * rows + 1] for p, o in zip(every, offsets))
    both = both * lax.rsqrt(variance + 1e-05)
    left_out[...] = both[:, :proj]
    both_buf[...] = both

    mine = lax.div(row, blocks) == col
    own = lax.rem(row, blocks)

    def row_copies():
        return [
            put(both_buf, right_buf.at[own], right_send.at[k], right_recv.at[own], {"row": peer})
            for k, peer in enumerate(row_peers)
        ]

    @pl.when(mine)
    def _():
        for copy in row_copies():
            copy.start()
        keep = pltpu.make_async_copy(both_buf, right_buf.at[own], right_recv.at[own])
        keep.start()
        keep.wait()

    def relay(j, block):
        slot = right_buf.at[block]
        return put(slot, slot, relay_send.at[j], right_recv.at[block], {"row": core_peer})

    for j in range(blocks // 2):
        block = 2 * j + core

        @pl.when(col * blocks + block != row)
        def _():
            relay(j, block).wait_recv()

        relay(j, block).start()
    for j in range(blocks // 2):
        relay(j, 2 * j + 1 - core).wait_recv()
    for b in range(blocks):
        right_out[b * rows : (b + 1) * rows] = right_buf[b][:, proj:]
    for j in range(blocks // 2):
        relay(j, 2 * j + core).wait_send()

    @pl.when(mine)
    def _():
        for copy in row_copies():
            copy.wait_send()


def merge(part, stat, seq, w_out, w_left, w_right, head_dim, heads, cols):
    n, n_col = lax.axis_size("row"), lax.axis_size("col")
    rows = seq.shape[0]
    proj = w_left.shape[1]
    blocks = cols // rows
    w_both = jnp.concatenate([w_left, w_right], axis=1)
    vmem = pl.BlockSpec(memory_space=pltpu.VMEM)
    dma = pltpu.SemaphoreType.DMA
    peers = n_col - 1
    return pl.pallas_call(
        functools.partial(merge_kernel, n, n_col, head_dim, heads),
        out_shape=(
            jax.ShapeDtypeStruct(seq.shape, F32),
            jax.ShapeDtypeStruct((rows, proj), F32),
            jax.ShapeDtypeStruct((cols, proj), F32),
        ),
        in_specs=[vmem] * 5,
        out_specs=(vmem,) * 3,
        scratch_shapes=[
            pltpu.VMEM((peers, *part.shape), F32),
            pltpu.VMEM((peers, *stat.shape), F32),
            pltpu.VMEM((2 * rows + 8, 2 * proj), F32),
            pltpu.VMEM((peers, 2 * rows + 8, 2 * proj), F32),
            pltpu.VMEM((rows, 2 * proj), F32),
            pltpu.VMEM((blocks, rows, 2 * proj), F32),
            dma((peers,)), dma((peers,)), dma((peers,)), dma((peers,)), dma((peers,)),
            dma((peers,)), dma((n // 2 - 1,)), dma((blocks,)), dma((blocks // 2,)),
        ],
        compiler_params=pltpu.CompilerParams(
            vmem_limit_bytes=VMEM_LIMIT, collective_id=1, has_side_effects=True
        ),
        name="merge",
    )(part, stat, seq, w_out, w_both)


def transition_kernel(
    pair_ref, left_ref, right_ref, w_outer_ref, bias_ref, w_up_ref, w_down_ref, out_ref,
    left_t, right_s, left_d, up_ref, down_ref, down_hi_ref,
):
    step = pl.program_id(0)
    group, cols, channels = pair_ref.shape
    proj = left_ref.shape[1]
    dot = functools.partial(jnp.dot, preferred_element_type=F32)

    @pl.when(step == 0)
    def _():
        left = left_ref[...]
        left_t[...] = left.T
        left_d[...] = jnp.dot(left, w_outer_ref[proj:], precision=HIGH) + bias_ref[...]
        r_hi, r_lo = halves(right_ref[...])
        right_s[...] = jnp.concatenate([r_hi, r_lo, r_hi], axis=1)
        up_hi, up_lo = halves(w_up_ref[...])
        up_ref[...] = jnp.concatenate([up_hi, up_hi, up_lo], axis=0)
        down_hi, down_lo = halves(w_down_ref[...])
        down_ref[...] = jnp.concatenate([down_hi, down_lo], axis=1)
        down_hi_ref[...] = down_hi

    lane = lax.broadcasted_iota(jnp.int32, left_t.shape, 1)
    w_prod = w_outer_ref[:proj]
    w_diff = w_outer_ref[proj:]
    weights = []
    for g in range(group):
        column = jnp.sum(
            jnp.where(lane == step * group + g, left_t[...], 0.0), axis=1, keepdims=True
        )
        w_hi, w_lo = halves(column * w_prod - w_diff)
        weights.append(jnp.concatenate([w_hi, w_hi, w_lo], axis=0))
    outer = dot(right_s[...], jnp.concatenate(weights, axis=1))
    for g in range(group):
        mid = pair_ref[g] + (
            outer[:, g * channels : (g + 1) * channels]
            + left_d[pl.ds(step * group + g, 1), :]
        )
        x_hi, x_lo = halves(channel_norm(mid))
        hidden = jnp.maximum(dot(jnp.concatenate([x_hi, x_lo, x_hi], axis=1), up_ref[...]), 0.0)
        h_hi, h_lo = halves(hidden)
        both = dot(h_hi, down_ref[...])
        out_ref[g] = mid + (
            both[:, :channels] + (both[:, channels:] + dot(h_lo, down_hi_ref[...]))
        )


def transition(pair, left, right, w_outer, outer_bias, w_up, w_down):
    rows, cols, channels = pair.shape
    proj = left.shape[1]
    hidden = w_up.shape[1]
    group = 4

    def whole(x):
        return pl.BlockSpec(x.shape, lambda i: (0,) * x.ndim)

    block = pl.BlockSpec((group, cols, channels), lambda i: (i, 0, 0))
    fixed = (left, right, w_outer, outer_bias.reshape(1, channels), w_up, w_down)
    return pl.pallas_call(
        transition_kernel,
        out_shape=jax.ShapeDtypeStruct(pair.shape, F32),
        grid=(rows // group,),
        in_specs=[block] + [whole(x) for x in fixed],
        out_specs=block,
        scratch_shapes=[
            pltpu.VMEM((proj, rows), F32),
            pltpu.VMEM((cols, 3 * proj), BF16),
            pltpu.VMEM((rows, channels), F32),
            pltpu.VMEM((3 * channels, hidden), BF16),
            pltpu.VMEM((hidden, 2 * channels), BF16),
            pltpu.VMEM((hidden, channels), BF16),
        ],
        compiler_params=pltpu.CompilerParams(vmem_limit_bytes=VMEM_LIMIT),
        name="transition",
    )(pair, *fixed)


def per_device(
    seq, query, key, value, pair, w_bias, w_out, w_left, w_right, w_outer, outer_bias, w_up, w_down
):
    rows, cols, channels = pair.shape
    heads = w_bias.shape[1]
    width = w_out.shape[0]
    head_dim = width // heads
    part, stat = gather_attention(query, key, value, pair, w_bias)
    seq_new, left, right = merge(
        part, stat, seq, w_out, w_left, w_right, head_dim, heads, cols
    )
    pair_new = transition(pair, left, right, w_outer, outer_bias, w_up, w_down)
    return seq_new, pair_new


def solution(mesh):
    in_specs = (
        P("row", "col"),
        P("row", "col"),
        P("col", "row"),
        P("col", "row"),
        P("row", "col", None),
        P(),
        P(None, "col"),
        P("col", None),
        P("col", None),
        P(),
        P(),
        P(),
        P(),
    )
    out_specs = (P("row", "col"), P("row", "col", None))
    return jax.shard_map(
        per_device, mesh=mesh, in_specs=in_specs, out_specs=out_specs, check_vma=False
    )
```
